32 devices in a mesh: replica: 4 (over y, x), fsdp: 8 (over z, core).
Axes of the slice: x: 2, y: 2, z: 4, core: 2. Of those that a mesh axis runs over, the one named last changes fastest.
Arguments:
- gradients: bfloat16 [4, 8192, 8192], P('replica', 'fsdp'), may hold values from -0.3984375 to 0.3984375
- projection: bfloat16 [8192, 512], P('fsdp'), may hold values from -0.25 to 0.25
- plan: int32 [256], replicated, may hold values from 0 to 255, each once
- first_codes: bfloat16 [8192, 512], P(('replica', 'fsdp')), may hold values from -1 to 1
- first_scales: float32 [8192, 2], P(('replica', 'fsdp')), may hold values from 0.02 to 0.08
- second_codes: bfloat16 [8192, 512], P(('replica', 'fsdp')), may hold values from 0.099609375 to 1
- second_scales: float32 [8192, 2], P(('replica', 'fsdp')), may hold values from 0.0001 to 0.0004
Outputs:
- update: bfloat16 [8192, 8192], P('fsdp')
- new_first_codes: bfloat16 [8192, 512], P(('replica', 'fsdp'))
- new_first_scales: float32 [8192, 2], P(('replica', 'fsdp'))
- new_second_codes: bfloat16 [8192, 512], P(('replica', 'fsdp'))
- new_second_scales: float32 [8192, 2], P(('replica', 'fsdp'))
The draws below stay inside these ranges and needn't reach their ends.
Inputs may be any that keep to these rules, and one draw needn't show every extreme that they name: `plan`: each of the 256 panels appears once.
All inputs are finite; a program needn't handle non-finite values. Where the reference program divides by a largest or mean magnitude, that divisor is 1e-20 or more.
Results may differ from the reference program's by a relative error of at most 0.014.
Values may be sent and summed in bfloat16 or wider, within the bound.
No kernel may reach another device: no remote copies, remote signals or barrier semaphores. Data moves between devices by JAX's collectives and lax.ppermute only.
A program may use at most 128 MiB of HBM per device.

```python
import math
import jax
import jax.numpy as jnp
from jax import lax

M = 8192
N = 8192
RANK = 512
PW = 32
QB = 256
STEP = 2
REPLICAS = 4
PANELS = 256
BLOCKS = 2


def levels(own_key, extent, cuts, smallest, high):
    def one(axis_at, blocks):
        heights = jax.random.uniform(jax.random.fold_in(jax.random.fold_in(own_key, 6), axis_at), (blocks,), jnp.float32, smallest / len(cuts), high / len(cuts))
        return jnp.repeat(jnp.exp(heights), extent[axis_at] // blocks).reshape((-1,) + (1,) * (len(extent) - axis_at - 1))

    gain = one(*cuts[0])
    for cut in cuts[1:]:
        gain = gain * one(*cut)
    return gain


def noise(rng, shape, spread, reach, cuts=(), kind=jnp.bfloat16):
    entries = jax.random.normal(rng, shape, jnp.float32) * spread
    if len(cuts) > 0:
        entries = levels(rng, shape, cuts, -0.22, 0.18) * entries
    return jnp.clip(entries, min=-reach, max=reach).astype(kind)


def setup_inputs(seed: int = 0) -> dict:
    arg_keys = jax.random.split(jax.random.key(seed), 8)
    return {
        "gradients": noise(arg_keys[0], (REPLICAS, M, N), 0.05, 0.3984375, ((0, 4), (1, 8))),
        "projection": noise(arg_keys[1], (M, RANK), RANK ** -0.5, 0.25, ((0, 8),)),
        "plan": jax.random.permutation(arg_keys[2], PANELS).astype(jnp.int32),
        "first_codes": jnp.clip(jax.random.uniform(arg_keys[3], (N, RANK), jnp.float32, -1.0, 1.0) * levels(arg_keys[3], (N, RANK), ((0, 32),), -0.4, 0.0), -1.0, 1.0).astype(jnp.bfloat16),
        "first_scales": jnp.clip(jnp.exp(math.log(0.08) - 1.3862944 * jax.random.uniform(arg_keys[4], (N, BLOCKS), jnp.float32) ** levels(arg_keys[4], (N, BLOCKS), ((0, 32),), -0.2, 0.2)), 0.02, 0.08),
        "second_codes": jnp.clip(0.099609375 + 0.9003906 * jax.random.uniform(arg_keys[5], (N, RANK), jnp.float32) ** levels(arg_keys[5], (N, RANK), ((0, 32),), -0.2, 0.2), 0.099609375, 1.0).astype(jnp.bfloat16),
        "second_scales": jnp.clip(jnp.exp(math.log(0.0004) - 1.3862944 * jax.random.uniform(arg_keys[6], (N, BLOCKS), jnp.float32) ** levels(arg_keys[6], (N, BLOCKS), ((0, 32),), -0.2, 0.2)), 0.0001, 0.0004),
    }


beta_one = 0.9
beta_two = 0.999
adam_eps = 1e-08
scale_eps = 1e-06

def expand(code_vals, scales):
    blocks = code_vals.astype(jnp.float32).reshape(code_vals.shape[0], -1, QB)
    return (blocks * scales[:, :, None]).reshape(code_vals.shape)

def requant(values):
    blocks = values.reshape(values.shape[0], -1, QB)
    peak = lax.optimization_barrier(jnp.max(jnp.abs(blocks), axis=2)) + scale_eps
    return ((blocks / peak[:, :, None]).reshape(values.shape).astype(jnp.bfloat16), peak)

def reference(gradients, projection, plan, first_codes, first_scales, second_codes, second_scales):
    summed = lax.optimization_barrier(jnp.sum(gradients.astype(jnp.float32), axis=0))
    column_ids = (plan[:, None] * PW + jnp.arange(PW, dtype=jnp.int32)[None, :]).reshape(-1).astype(jnp.int32)
    picked = jnp.take(summed, column_ids, axis=1)
    lowrank = lax.dot_general(picked, projection.astype(jnp.float32), (((0,), (0,)), ((), ())), precision=lax.Precision.HIGHEST)
    first = expand(first_codes, first_scales)
    second = expand(second_codes, second_scales)
    first_new = beta_one * first + (1.0 - beta_one) * lowrank
    second_new = beta_two * second + (1.0 - beta_two) * lowrank * lowrank
    corr_one = 1.0 - beta_one ** STEP
    corr_two = 1.0 - beta_two ** STEP
    direction = (first_new / corr_one / (jnp.sqrt(second_new / corr_two) + adam_eps)).astype(jnp.bfloat16)
    first_out, first_peak = requant(first_new)
    second_out, second_peak = requant(second_new)
    natural = jnp.zeros((N, RANK), jnp.bfloat16).at[column_ids].set(direction)
    update = lax.dot_general(projection, natural, (((1,), (1,)), ((), ())), preferred_element_type=jnp.float32).astype(jnp.bfloat16)
    return (update, first_out, first_peak, second_out, second_peak)
```

```python
import functools

import jax
import jax.numpy as jnp
from jax import lax
from jax.experimental import pallas as pl
from jax.experimental.pallas import tpu as pltpu
from jax.sharding import PartitionSpec as P

PW = 32
QB = 256
STEP = 2


beta_one = 0.9
beta_two = 0.999
adam_eps = 1e-08
scale_eps = 1e-06


BOTH = ("replica", "fsdp")
VMEM_LIMIT = 56 * 1024 * 1024


def project_kernel(table, grad, proj, keep, send, block, sems):
    step = pl.program_id(0)
    slot = lax.rem(step, 2)
    half = keep.shape[0]
    panels = block.shape[1] // PW
    part = lax.dot_general(
        grad[0], proj[...], (((0,), (0,)), ((), ())), preferred_element_type=jnp.float32
    ).astype(jnp.bfloat16)

    def drain(which):
        pltpu.make_async_copy(block.at[which], block.at[which], sems.at[which]).wait()

    @pl.when(step >= 2)
    def _():
        drain(slot)

    block[slot] = part
    for k in range(panels):
        target = table[step * panels + k]
        source = block.at[slot, pl.ds(k * PW, PW)]

        @pl.when(target < half)
        def _():
            row = pl.multiple_of(target, PW)
            pltpu.make_async_copy(source, keep.at[pl.ds(row, PW)], sems.at[slot]).start()

        @pl.when(target >= half)
        def _():
            row = pl.multiple_of(target - half, PW)
            pltpu.make_async_copy(source, send.at[pl.ds(row, PW)], sems.at[slot]).start()

    @pl.when(step == pl.num_programs(0) - 1)
    def _():
        drain(slot)
        drain(1 - slot)


def project(table, gradients, projection, sub):
    rows, cols = gradients.shape[1:]
    width = min(512, cols // 2)
    half = jax.ShapeDtypeStruct((cols // 2, QB), jnp.bfloat16)
    return pl.pallas_call(
        project_kernel,
        out_shape=(half, half),
        grid_spec=pltpu.PrefetchScalarGridSpec(
            num_scalar_prefetch=1,
            grid=(cols // width,),
            in_specs=[
                pl.BlockSpec((1, rows, width), lambda j, t: (0, 0, j)),
                pl.BlockSpec((rows, QB), lambda j, t: (0, sub)),
            ],
            out_specs=[pl.BlockSpec(memory_space=pl.ANY)] * 2,
            scratch_shapes=[
                pltpu.VMEM((2, width, QB), jnp.bfloat16),
                pltpu.SemaphoreType.DMA((2,)),
            ],
        ),
        compiler_params=pltpu.CompilerParams(vmem_limit_bytes=VMEM_LIMIT),
        cost_estimate=pl.CostEstimate(
            flops=2 * rows * cols * QB,
            bytes_accessed=2 * (rows * cols + rows * QB + cols * QB),
            transcendentals=0,
        ),
        name="project",
    )(table, gradients, projection)


def moments_kernel(n_in, *refs):
    parts, (codes1, scales1, codes2, scales2) = refs[:n_in], refs[n_in : n_in + 4]
    direction, out1, peak1, out2, peak2 = refs[n_in + 4 :]
    lowrank = parts[0][...]
    for part in parts[1:]:
        lowrank = lowrank + part[...].astype(jnp.float32)

    def column(scales):
        rows = jnp.broadcast_to(scales[0], (8, scales.shape[2]))
        return jnp.transpose(rows)[:, :1]

    first = codes1[...].astype(jnp.float32) * column(scales1)
    second = codes2[...].astype(jnp.float32) * column(scales2)
    first_new = beta_one * first + (1.0 - beta_one) * lowrank
    second_new = beta_two * second + (1.0 - beta_two) * lowrank * lowrank
    corr_one = 1.0 - beta_one**STEP
    corr_two = 1.0 - beta_two**STEP
    direction[...] = (
        first_new / corr_one / (jnp.sqrt(second_new / corr_two) + adam_eps)
    ).astype(jnp.bfloat16)
    for values, out, peak_out in ((first_new, out1, peak1), (second_new, out2, peak2)):
        peak = jnp.max(jnp.abs(values), axis=1, keepdims=True) + scale_eps
        out[...] = (values / peak).astype(jnp.bfloat16)
        peak_out[0] = jnp.transpose(jnp.broadcast_to(peak, (peak.shape[0], 128)))[:1]


def moments(parts, codes1, scales1, codes2, scales2, sub):
    rows = codes1.shape[0]
    whole = pl.BlockSpec((rows, QB), lambda i: (0, 0))
    code = pl.BlockSpec((rows, QB), lambda i: (0, sub))
    scale = pl.BlockSpec((1, 1, rows), lambda i: (sub, 0, 0))
    peak = pl.BlockSpec((1, 1, rows), lambda i: (0, 0, 0))
    values = jax.ShapeDtypeStruct((rows, QB), jnp.bfloat16)
    peaks = jax.ShapeDtypeStruct((1, 1, rows), jnp.float32)
    return pl.pallas_call(
        functools.partial(moments_kernel, len(parts)),
        out_shape=(values, values, peaks, values, peaks),
        grid=(1,),
        in_specs=[whole] * len(parts) + [code, scale, code, scale],
        out_specs=[whole, whole, peak, whole, peak],
        cost_estimate=pl.CostEstimate(
            flops=30 * rows * QB, bytes_accessed=20 * rows * QB, transcendentals=rows * QB
        ),
        name="moments",
    )(*parts, codes1, scales1, codes2, scales2)


def update_kernel(places, table, proj, *refs):
    pieces, out, held, natural, sem = refs[:-4], refs[-4], refs[-3], refs[-2], refs[-1]
    step = pl.program_id(0)
    width = natural.shape[0]
    panels = width // PW

    @pl.when(step == 0)
    def _():
        copies = [
            pltpu.make_async_copy(
                pieces[piece].at[pl.ds(start, size)], held.at[sub, pl.ds(row, size)], sem.at[n]
            )
            for n, (piece, start, size, sub, row) in enumerate(places)
        ]
        for copy in copies:
            copy.start()
        for copy in copies:
            copy.wait()

    for k in range(panels):
        row = pl.multiple_of(table[step * panels + k], PW)
        for sub in range(held.shape[0]):
            natural[k * PW : (k + 1) * PW, sub * QB : (sub + 1) * QB] = held[
                sub, pl.ds(row, PW), :
            ]
    out[...] = lax.dot_general(
        proj[...], natural[...], (((1,), (1,)), ((), ())), preferred_element_type=jnp.float32
    ).astype(jnp.bfloat16)


def back_project(table, projection, pieces, places, cols):
    rows, rank = projection.shape
    width = min(512, cols)
    return pl.pallas_call(
        functools.partial(update_kernel, places),
        out_shape=jax.ShapeDtypeStruct((rows, cols), jnp.bfloat16),
        grid_spec=pltpu.PrefetchScalarGridSpec(
            num_scalar_prefetch=1,
            grid=(cols // width,),
            in_specs=[pl.BlockSpec((rows, rank), lambda j, t: (0, 0))]
            + [pl.BlockSpec(memory_space=pl.ANY)] * len(pieces),
            out_specs=pl.BlockSpec((rows, width), lambda j, t: (0, j)),
            scratch_shapes=[
                pltpu.VMEM((rank // QB, cols, QB), jnp.bfloat16),
                pltpu.VMEM((width, rank), jnp.bfloat16),
                pltpu.SemaphoreType.DMA((len(places),)),
            ],
        ),
        compiler_params=pltpu.CompilerParams(vmem_limit_bytes=VMEM_LIMIT),
        cost_estimate=pl.CostEstimate(
            flops=2 * rows * cols * rank,
            bytes_accessed=2 * (rows * cols + rows * rank + cols * rank),
            transcendentals=0,
        ),
        name="back_project",
    )(table, projection, *pieces)


def solution(mesh):
    n_rep, n_fsdp = mesh.shape["replica"], mesh.shape["fsdp"]
    n_core = 2
    n_z = n_fsdp // n_core
    bits = n_rep.bit_length() - 1

    def swap(x, rep=0, z=0, core=0):
        perm = []
        for r in range(n_rep):
            for f in range(n_fsdp):
                other = (f // n_core ^ z) * n_core + (f % n_core ^ core)
                perm.append((r * n_fsdp + f, (r ^ rep) * n_fsdp + other))
        return lax.ppermute(x, BOTH, perm)

    def reduce_color(terms, order, lead):
        left = list(range(bits))
        for bit in order:
            axis = left.index(bit)
            far = [lax.index_in_dim(t, 1, axis, keepdims=False) for t in terms]
            near = [lax.index_in_dim(t, 0, axis, keepdims=False) for t in terms]
            out = sum(t.astype(jnp.float32) for t in far).astype(jnp.bfloat16)
            terms = near + [swap(out, rep=1 << (bits - 1 - bit))]
            left.remove(bit)
        return terms

    def local(gradients, projection, plan, first_codes, first_scales, second_codes, second_scales):
        cols = gradients.shape[2]
        rank = projection.shape[1]
        subs = rank // QB
        rows = first_codes.shape[0]
        part = rows // 2
        per = rows // PW
        spots = jnp.arange(cols // PW, dtype=jnp.int32)
        device, spot = spots // per, spots % per
        rep, fs = device // n_fsdp, device % n_fsdp
        me_r, me_f = lax.axis_index("replica"), lax.axis_index("fsdp")
        rep = rep ^ me_r
        z = (fs // n_core) ^ (me_f // n_core)
        core = (fs % n_core) ^ (me_f % n_core)
        color, spot = spot // (per // 2), spot % (per // 2)
        place = (((core * 2 + color) * n_rep + rep) * n_z + z) * part + spot * PW
        table = jnp.sum(
            jnp.where(plan[:, None] == spots[None, :], place[:, None], 0), axis=0, dtype=jnp.int32
        )
        orders = [list(range(bits)), list(range(bits))[::-1]]

        halves = [project(table, gradients, projection, sub) for sub in range(subs)]
        scales1 = first_scales.T.reshape(subs, 1, rows)
        scales2 = second_scales.T.reshape(subs, 1, rows)
        shape = (2,) + (2,) * bits + (n_z * part, QB)
        results, pieces, places = [], [], []
        for sub, (keep, send) in enumerate(halves):
            got = swap(send, core=1).reshape(shape)
            keep = keep.reshape(shape)
            sums = []
            for c in range(2):
                terms = reduce_color([keep[c], got[c]], orders[c], None)
                sums.append([t.reshape(n_z, part, QB) for t in terms])

            def total(k):
                return jnp.concatenate(
                    [sum(t[k].astype(jnp.float32) for t in terms) for terms in sums]
                )

            parts = [total(0)]
            for k in range(1, n_z):
                parts.append(swap(total(k).astype(jnp.bfloat16), z=k))
            direction, out1, peak1, out2, peak2 = moments(
                parts, first_codes, scales1, second_codes, scales2, sub
            )
            results.append((out1, peak1, out2, peak2))
            blocks = [direction] + [swap(direction, z=k) for k in range(1, n_z)]
            for c in range(2):
                whole = jnp.concatenate([b[c * part : (c + 1) * part] for b in blocks])
                ranks = [0]
                for n, bit in enumerate(orders[c][::-1]):
                    flip = 1 << (bits - 1 - bit)
                    there = swap(whole, rep=flip)
                    if n < bits - 1:
                        whole = jnp.concatenate([whole, there])
                        ranks = ranks + [r + flip for r in ranks]
                for arr, rs in ((whole, ranks), (there, [r + flip for r in ranks])):
                    for k, piece in enumerate((arr, swap(arr, core=1))):
                        for n, r in enumerate(rs):
                            row = ((k * 2 + c) * n_rep + r) * n_z * part
                            places.append((len(pieces), n * n_z * part, n_z * part, sub, row))
                        pieces.append(piece)
        update = back_project(table, projection, pieces, tuple(places), cols)
        out1 = jnp.concatenate([r[0] for r in results], axis=1)
        out2 = jnp.concatenate([r[2] for r in results], axis=1)
        peak1 = jnp.concatenate([r[1].reshape(1, rows) for r in results]).T
        peak2 = jnp.concatenate([r[3].reshape(1, rows) for r in results]).T
        return (update, out1, peak1, out2, peak2)

    split = P(BOTH, None)
    in_specs = (P("replica", "fsdp", None), P("fsdp", None), P(), split, split, split, split)
    out_specs = (P("fsdp", None), split, split, split, split)
    return jax.shard_map(local, mesh=mesh, in_specs=in_specs, out_specs=out_specs, check_vma=False)
```

```python
import functools

import jax
import jax.numpy as jnp
from jax import lax
from jax.experimental import pallas as pl
from jax.experimental.pallas import tpu as pltpu
from jax.sharding import PartitionSpec as P


PW = 32
QB = 256
STEP = 2


beta_one = 0.9
beta_two = 0.999
adam_eps = 1e-08
scale_eps = 1e-06


BOTH = ("replica", "fsdp")
VMEM_LIMIT = 32 * 1024 * 1024
PROJECT_LIMIT = 44 * 1024 * 1024


def project_kernel(table, grad, proj, out):
    step = pl.program_id(0)
    panels = grad.shape[2] // PW
    part = lax.dot_general(
        grad[0], proj[...], (((0,), (0,)), ((), ())), preferred_element_type=jnp.float32
    ).astype(jnp.bfloat16)
    for k in range(panels):
        row = pl.multiple_of(table[step * panels + k], PW)
        out[pl.ds(row, PW), :] = part[k * PW : (k + 1) * PW]


def project(table, gradients, projection, sub):
    rows, cols = gradients.shape[1:]
    width = min(1024, cols)
    return pl.pallas_call(
        project_kernel,
        out_shape=jax.ShapeDtypeStruct((cols, QB), jnp.bfloat16),
        grid_spec=pltpu.PrefetchScalarGridSpec(
            num_scalar_prefetch=1,
            grid=(cols // width,),
            in_specs=[
                pl.BlockSpec((1, rows, width), lambda j, t: (0, 0, j)),
                pl.BlockSpec((rows, QB), lambda j, t: (0, sub)),
            ],
            out_specs=pl.BlockSpec(memory_space=pltpu.VMEM),
        ),
        compiler_params=pltpu.CompilerParams(vmem_limit_bytes=PROJECT_LIMIT),
        cost_estimate=pl.CostEstimate(
            flops=2 * rows * cols * QB,
            bytes_accessed=2 * (rows * cols + rows * QB + cols * QB),
            transcendentals=0,
        ),
        name="project",
    )(table, gradients, projection)


def moments_kernel(sub, lowrank_ref, codes1, scales1, codes2, scales2, *refs):
    before, (direction, out1, peak1, out2, peak2) = refs[:-5], refs[-5:]
    lowrank = lowrank_ref[...]
    block = slice(sub * QB, (sub + 1) * QB)
    for old, new in zip(before, (out1, peak1, out2, peak2)):
        if old.shape[0] == lowrank.shape[0]:
            new[:, : old.shape[1]] = old[...]
        else:
            new[: old.shape[0]] = old[...]

    def column(scales):
        rows = jnp.broadcast_to(scales[sub : sub + 1, :], (8, scales.shape[1]))
        return jnp.transpose(rows)[:, :1]

    first = codes1[:, block].astype(jnp.float32) * column(scales1)
    second = codes2[:, block].astype(jnp.float32) * column(scales2)
    first_new = beta_one * first + (1.0 - beta_one) * lowrank
    second_new = beta_two * second + (1.0 - beta_two) * lowrank * lowrank
    corr_one = 1.0 - beta_one**STEP
    corr_two = 1.0 - beta_two**STEP
    direction[...] = (
        first_new / corr_one / (jnp.sqrt(second_new / corr_two) + adam_eps)
    ).astype(jnp.bfloat16)
    for values, out, peak_out in ((first_new, out1, peak1), (second_new, out2, peak2)):
        peak = jnp.max(jnp.abs(values), axis=1, keepdims=True) + scale_eps
        out[:, block] = (values / peak).astype(jnp.bfloat16)
        peak_out[sub : sub + 1] = jnp.transpose(
            jnp.broadcast_to(peak, (peak.shape[0], 128))
        )[:1]


def moments(lowrank, codes1, scales1, codes2, scales2, sub, before):
    rows = codes1.shape[0]
    vmem = pl.BlockSpec(memory_space=pltpu.VMEM)
    direction = jax.ShapeDtypeStruct((rows, QB), jnp.bfloat16)
    values = jax.ShapeDtypeStruct((rows, (sub + 1) * QB), jnp.bfloat16)
    peaks = jax.ShapeDtypeStruct((sub + 1, rows), jnp.float32)
    return pl.pallas_call(
        functools.partial(moments_kernel, sub),
        out_shape=(direction, values, peaks, values, peaks),
        in_specs=[vmem] * (5 + len(before)),
        out_specs=[vmem] * 5,
        compiler_params=pltpu.CompilerParams(vmem_limit_bytes=8 * 1024 * 1024),
        cost_estimate=pl.CostEstimate(
            flops=30 * rows * QB, bytes_accessed=20 * rows * QB, transcendentals=rows * QB
        ),
        name="moments",
    )(lowrank, codes1, scales1, codes2, scales2, *before)


def update_kernel(places, table, proj, *refs):
    pieces, out, held, natural, sem = refs[:-4], refs[-4], refs[-3], refs[-2], refs[-1]
    step = pl.program_id(0)
    width = natural.shape[0]
    panels = width // PW

    @pl.when(step == 0)
    def _():
        copies = [
            pltpu.make_async_copy(
                pieces[piece].at[pl.ds(start, size)], held.at[sub, pl.ds(row, size)], sem.at[n]
            )
            for n, (piece, start, size, sub, row) in enumerate(places)
        ]
        for copy in copies:
            copy.start()
        for copy in copies:
            copy.wait()

    for k in range(panels):
        row = pl.multiple_of(table[step * panels + k], PW)
        for sub in range(held.shape[0]):
            natural[k * PW : (k + 1) * PW, sub * QB : (sub + 1) * QB] = held[
                sub, pl.ds(row, PW), :
            ]
    out[...] = lax.dot_general(
        proj[...], natural[...], (((1,), (1,)), ((), ())), preferred_element_type=jnp.float32
    ).astype(jnp.bfloat16)


def back_project(table, projection, pieces, places, cols):
    rows, rank = projection.shape
    width = min(1024, cols)
    return pl.pallas_call(
        functools.partial(update_kernel, places),
        out_shape=jax.ShapeDtypeStruct((rows, cols), jnp.bfloat16),
        grid_spec=pltpu.PrefetchScalarGridSpec(
            num_scalar_prefetch=1,
            grid=(cols // width,),
            in_specs=[pl.BlockSpec((rows, rank), lambda j, t: (0, 0))]
            + [pl.BlockSpec(memory_space=pl.ANY)] * len(pieces),
            out_specs=pl.BlockSpec((rows, width), lambda j, t: (0, j)),
            scratch_shapes=[
                pltpu.VMEM((rank // QB, cols, QB), jnp.bfloat16),
                pltpu.VMEM((width, rank), jnp.bfloat16),
                pltpu.SemaphoreType.DMA((len(places),)),
            ],
        ),
        compiler_params=pltpu.CompilerParams(vmem_limit_bytes=VMEM_LIMIT),
        cost_estimate=pl.CostEstimate(
            flops=2 * rows * cols * rank,
            bytes_accessed=2 * (rows * cols + rows * rank + cols * rank),
            transcendentals=0,
        ),
        name="back_project",
    )(table, projection, *pieces)


def add(terms):
    return sum(t.astype(jnp.float32) for t in terms)


def solution(mesh):
    n_rep, n_fsdp = mesh.shape["replica"], mesh.shape["fsdp"]
    n_core = 2
    n_z = n_fsdp // n_core
    r_bits, z_bits = n_rep.bit_length() - 1, n_z.bit_length() - 1
    orders = [list(range(r_bits)), list(range(r_bits))[::-1]]

    def spot_of(r):
        return sum(((r >> b) & 1) << (r_bits - 1 - b) for b in range(r_bits))

    def swap(x, rep=0, z=0, core=0):
        perm = []
        for r in range(n_rep):
            for f in range(n_fsdp):
                other = (f // n_core ^ z) * n_core + (f % n_core ^ core)
                perm.append((r * n_fsdp + f, (r ^ rep) * n_fsdp + other))
        return lax.ppermute(x, BOTH, perm)

    def stream(sub, keep, send, update_moments, results, pieces, places):
        part = keep.shape[0] // (2 * n_rep * n_z)
        shape = (2,) + (2,) * (r_bits + z_bits) + (part, QB)
        got = swap(send, core=1).reshape(shape)
        yield
        keep = keep.reshape(shape)
        terms = [[keep[c], got[c]] for c in range(2)]
        left = [list(range(r_bits)), list(range(r_bits))]
        for n in range(r_bits):
            for c in range(2):
                bit = orders[c][n]
                axis = left[c].index(bit)
                far = [lax.index_in_dim(t, 1, axis, keepdims=False) for t in terms[c]]
                near = [lax.index_in_dim(t, 0, axis, keepdims=False) for t in terms[c]]
                terms[c] = near + [swap(add(far).astype(jnp.bfloat16), rep=1 << bit)]
                left[c].remove(bit)
            yield
        for bit in range(z_bits):
            far = jnp.stack([add([t[1] for t in terms[c]]) for c in range(2)])
            got = swap(far.astype(jnp.bfloat16), z=1 << bit)
            terms = [[t[0] for t in terms[c]] + [got[c]] for c in range(2)]
            yield
        lowrank = jnp.concatenate([add(terms[c]) for c in range(2)])
        direction, *rest = update_moments(lowrank)
        results[:] = rest
        blocks = direction.reshape(1, 2, part, QB)
        for bit in range(z_bits)[::-1]:
            blocks = jnp.concatenate([blocks, swap(blocks, z=1 << bit)])
            yield
        whole = [blocks[:, c].reshape(n_z * part, QB) for c in range(2)]
        there, ranks = [None, None], [[0], [0]]
        for n in range(r_bits):
            for c in range(2):
                flip = 1 << orders[c][::-1][n]
                if n > 0:
                    whole[c] = jnp.concatenate([whole[c], there[c]])
                there[c] = swap(whole[c], rep=flip)
                ranks[c] = ranks[c] + [r + flip for r in ranks[c]]
            yield
        for late, group in enumerate((whole, there)):
            for c in range(2):
                size = group[c].shape[0] // (n_z * part)
                mine = ranks[c][late * size : (late + 1) * size]
                for k, piece in enumerate((group[c], swap(group[c], core=1))):
                    for n, r in enumerate(mine):
                        row = ((k * 2 + c) * n_rep + spot_of(r)) * n_z * part
                        places.append((len(pieces), n * n_z * part, n_z * part, sub, row))
                    pieces.append(piece)
            yield

    def local(gradients, projection, plan, first_codes, first_scales, second_codes, second_scales):
        cols = gradients.shape[2]
        rank = projection.shape[1]
        subs = rank // QB
        rows = first_codes.shape[0]
        part = rows // 2
        per = rows // PW
        spots = jnp.arange(cols // PW, dtype=jnp.int32)
        device, spot = spots // per, spots % per
        rep, fs = device // n_fsdp, device % n_fsdp
        me_r, me_f = lax.axis_index("replica"), lax.axis_index("fsdp")
        rep = rep ^ me_r
        z = (fs // n_core) ^ (me_f // n_core)
        core = (fs % n_core) ^ (me_f % n_core)
        rep = sum(((rep >> b) & 1) << (r_bits - 1 - b) for b in range(r_bits))
        z = sum(((z >> b) & 1) << (z_bits - 1 - b) for b in range(z_bits))
        color, spot = spot // (per // 2), spot % (per // 2)
        place = (((core * 2 + color) * n_rep + rep) * n_z + z) * part + spot * PW
        place = lax.optimization_barrier(place)
        table = jnp.sum(
            jnp.where(plan[:, None] == spots[None, :], place[:, None], 0), axis=0, dtype=jnp.int32
        )
        scales1, scales2 = first_scales.T, second_scales.T
        results, pieces, places = [], [], []
        streams = []
        for sub in range(subs):
            both = project(table, gradients, projection, sub)
            keep, send = both[: cols // 2], both[cols // 2 :]

            def update_moments(lowrank, sub=sub):
                return moments(
                    lowrank, first_codes, scales1, second_codes, scales2, sub, tuple(results)
                )

            streams.append(
                stream(sub, keep, send, update_moments, results, pieces, places)
            )
        phases = 1 + 2 * r_bits + 2 * z_bits + 2
        order = sorted(
            (p + sub * (1.5 if p < r_bits else 2.5) + (phases if p >= phases - 2 else 0), sub)
            for sub in range(subs)
            for p in range(phases)
        )
        for _, sub in order:
            next(streams[sub])
        update = back_project(table, projection, pieces, tuple(places), cols)
        out1, peak1, out2, peak2 = results
        return (update, out1, peak1.T, out2, peak2.T)

    split = P(BOTH, None)
    in_specs = (P("replica", "fsdp", None), P("fsdp", None), P(), split, split, split, split)
    out_specs = (P("fsdp", None), split, split, split, split)
    return jax.shard_map(local, mesh=mesh, in_specs=in_specs, out_specs=out_specs, check_vma=False)
```
